256 devices in a mesh: band: 16 (over z, y_lo), pw: 16 (over x, y_hi, core).
Axes of the slice: x: 4, y: 4 (y_hi: 2, y_lo: 2; y = y_hi * 2 + y_lo), z: 8, core: 2. Of those that a mesh axis runs over, the one named last changes fastest.
Arguments:
- orbitals: bfloat16 [32, 192, 192, 256], P('band', 'pw'), may hold values from -5 to 5
- owner_group: int32 [1], replicated, may hold values from 0 to 15
Outputs:
- exchange_rows: float32 [32, 192, 192, 256], P('band', 'pw')
- owner_update: float32 [1, 192, 192, 256], P(None, 'pw', 'band')
The draws below stay inside these ranges and needn't reach their ends.
All inputs are finite; a program needn't handle non-finite values.
Results may differ from the reference program's by a relative error of at most 0.0003.
Values may be sent and summed in bfloat16 or wider, within the bound.
A program may use at most 128 MiB of HBM per device.

```python
import math
import jax
import jax.numpy as jnp
from jax import lax

NX = 192
NY = 192
NZ = 256
OWN = 2
SENT = 1
NBANDS = 32
N_BAND = 16


def draw_orbitals(key, part):
    full_shape = (NBANDS, NX, NY, NZ)
    return jnp.clip(jax.random.normal(key, full_shape, jnp.float32), -5.0, 5.0).astype(jnp.bfloat16)


def setup_inputs(seed: int = 0) -> dict:
    splits = jax.random.split(jax.random.key(seed), 3)
    orbitals = draw_orbitals(jax.random.fold_in(splits[2], 71), 0)
    owner_group = jax.random.randint(splits[1], (1,), 0, N_BAND).astype(jnp.int32)
    return dict(orbitals=orbitals, owner_group=owner_group)


exact_share = 0.25
spacing = 0.2


def coulomb_table(ky_first, rows_y):
    freq_x = jnp.arange(NX, dtype=jnp.int32)
    freq_x = jnp.where(freq_x > NX // 2, freq_x - NX, freq_x)
    freq_y = ky_first + jnp.arange(rows_y, dtype=jnp.int32)
    freq_y = jnp.where(freq_y > NY // 2, freq_y - NY, freq_y)
    freq_z = jnp.arange(NZ // 2 + 1, dtype=jnp.int32)
    wave_x = freq_x.astype(jnp.float32) * (2 * math.pi / (NX * spacing))
    wave_y = freq_y.astype(jnp.float32) * (2 * math.pi / (NY * spacing))
    wave_z = freq_z.astype(jnp.float32) * (2 * math.pi / (NZ * spacing))
    square = (wave_x * wave_x)[:, None, None] + (wave_y * wave_y)[None, :, None] + (wave_z * wave_z)[None, None, :]
    safe = jnp.where(square > 0, square, 1.0)
    return jnp.where(square > 0, 4 * math.pi / safe, 0.0)


def reference(orbitals, owner_group):
    kernel = coulomb_table(0, NY)
    first_band = (owner_group[0] * OWN).astype(jnp.int32)
    sent_values = lax.dynamic_slice_in_dim(orbitals, first_band, SENT, 0).astype(jnp.float32)
    grouped = orbitals.reshape(N_BAND, OWN, NX, NY, NZ)

    def one_group(update_sum, block):
        own_values = block.astype(jnp.float32)
        rows_out = []
        for own_index in range(OWN):
            total = jnp.zeros((NX, NY, NZ), jnp.float32)
            for sent_index in range(SENT):
                density = own_values[own_index] * sent_values[sent_index]
                potential = jnp.fft.irfftn(kernel * jnp.fft.rfftn(density), s=(NX, NY, NZ))
                total = total - exact_share * sent_values[sent_index] * potential
                update_sum = update_sum.at[sent_index].add(-exact_share * own_values[own_index] * potential)
            rows_out.append(total)
        return update_sum, jnp.stack(rows_out)

    zero_sum = jnp.zeros((SENT, NX, NY, NZ), jnp.float32)
    update, exchange = lax.scan(one_group, zero_sum, grouped)
    return exchange.reshape(OWN * N_BAND, NX, NY, NZ), update
```

```python
import math

import jax
import jax.numpy as jnp
from jax import lax
from jax.sharding import PartitionSpec as P

SENT = 1
CHUNKS = 4

exact_share = 0.25
spacing = 0.2
highest = lax.Precision.HIGHEST


def dft_tables(length, number):
    samples = jnp.arange(length, dtype=jnp.int32)
    frequency = jnp.arange(number, dtype=jnp.int32)
    phase_index = samples[:, None] * frequency[None, :] % length
    phase_angle = phase_index.astype(jnp.float32) * (2 * math.pi / length)
    return (jnp.cos(phase_angle), jnp.sin(phase_angle))


def signed(freq, length):
    return jnp.where(freq > length // 2, freq - length, freq)


def coulomb_table(nx, ny, nz, ky_first, rows_y, kz_first, cols_z):
    freq_x = signed(jnp.arange(nx, dtype=jnp.int32), nx)
    freq_y = signed(ky_first + jnp.arange(rows_y, dtype=jnp.int32), ny)
    freq_z = signed(kz_first + jnp.arange(cols_z, dtype=jnp.int32), nz)
    wave_x = freq_x.astype(jnp.float32) * (2 * math.pi / (nx * spacing))
    wave_y = freq_y.astype(jnp.float32) * (2 * math.pi / (ny * spacing))
    wave_z = freq_z.astype(jnp.float32) * (2 * math.pi / (nz * spacing))
    square = (
        (wave_x * wave_x)[:, None, None]
        + (wave_y * wave_y)[None, :, None]
        + (wave_z * wave_z)[None, None, :]
    )
    safe = jnp.where(square > 0, square, 1.0)
    return jnp.where(square > 0, 4 * math.pi / safe, 0.0)


def complex_pass(spectrum, cosine_table, sine_table, pattern, direction):
    half_width = spectrum.shape[-1] // 2
    with_cosine = jnp.einsum(pattern, cosine_table, spectrum, precision=highest)
    with_sine = jnp.einsum(pattern, sine_table, spectrum, precision=highest)
    real_part = with_cosine[..., :half_width] + direction * with_sine[..., half_width:]
    imag_part = with_cosine[..., half_width:] - direction * with_sine[..., :half_width]
    return jnp.concatenate([real_part, imag_part], -1)


def band_broadcast(block, owner, groups):
    rows = block.shape[0] * block.shape[1]
    pieces = block.reshape(groups, rows // groups, block.shape[2])
    received = lax.all_to_all(pieces, "band", 0, 0, tiled=True)
    mine = lax.dynamic_index_in_dim(received, owner, 0, keepdims=True)
    spread = jnp.broadcast_to(mine, pieces.shape)
    gathered = lax.all_to_all(spread, "band", 0, 0, tiled=True)
    return gathered.reshape(block.shape)


def band_reduce_scatter(partial, groups):
    slab_rows, ny, nz = partial.shape
    pieces = partial.reshape(slab_rows, groups, ny // groups, nz).transpose(1, 0, 2, 3)
    received = lax.all_to_all(pieces, "band", 0, 0, tiled=True)
    return jnp.sum(received, 0)


def on_device(orbitals, owner_group):
    slab_rows, ny, nz = orbitals.shape[1:]
    pw_size = lax.axis_size("pw")
    groups = lax.axis_size("band")
    nx = slab_rows * pw_size
    rows_y = ny // pw_size
    ky_first = lax.axis_index("pw") * rows_y
    width = nz // CHUNKS

    sent_values = band_broadcast(orbitals[0], owner_group[0], groups).astype(jnp.float32)
    own_values = orbitals.astype(jnp.float32)
    packed = jnp.concatenate(
        [own_values[0] * sent_values, own_values[1] * sent_values], -1
    )

    cosine_z, sine_z = dft_tables(nz, nz)
    forward_z = jnp.concatenate(
        [jnp.concatenate([cosine_z, -sine_z], 1), jnp.concatenate([sine_z, cosine_z], 1)], 0
    )
    scale = 1.0 / (nx * ny * nz)
    inverse_z = jnp.concatenate(
        [jnp.concatenate([cosine_z, sine_z], 1), jnp.concatenate([-sine_z, cosine_z], 1)], 0
    ) * scale
    cosine_y, sine_y = dft_tables(ny, ny)
    cosine_x, sine_x = dft_tables(nx, nx)

    result = None
    for chunk in range(CHUNKS):
        low = chunk * width
        columns = jnp.concatenate(
            [forward_z[:, low : low + width], forward_z[:, nz + low : nz + low + width]], 1
        )
        spectrum = jnp.einsum("xyz,zc->xyc", packed, columns, precision=highest)
        spectrum = complex_pass(spectrum, cosine_y, sine_y, "uy,xyc->xuc", 1.0)
        spectrum = lax.all_to_all(spectrum, "pw", 1, 0, tiled=True)
        spectrum = complex_pass(spectrum, cosine_x, sine_x, "ux,xyc->uyc", 1.0)
        kernel = coulomb_table(nx, ny, nz, ky_first, rows_y, low, width)
        spectrum = spectrum * jnp.concatenate([kernel, kernel], -1)
        spectrum = complex_pass(spectrum, cosine_x, sine_x, "ux,xyc->uyc", -1.0)
        spectrum = lax.all_to_all(spectrum, "pw", 0, 1, tiled=True)
        spectrum = complex_pass(spectrum, cosine_y, sine_y, "uy,xyc->xuc", -1.0)
        rows = jnp.concatenate(
            [inverse_z[low : low + width], inverse_z[nz + low : nz + low + width]], 0
        )
        part = jnp.einsum("xyc,cz->xyz", spectrum, rows, precision=highest)
        result = part if result is None else result + part

    potential = jnp.stack([result[..., :nz], result[..., nz:]])
    exchange_rows = -exact_share * (potential * sent_values[None])
    partial_value = -exact_share * jnp.sum(potential * own_values, 0)
    owner_update = band_reduce_scatter(partial_value, groups)[None]
    return (exchange_rows, owner_update)


def solution(mesh):
    placed = (P("band", "pw", None, None), P())
    return jax.shard_map(
        on_device,
        mesh=mesh,
        in_specs=placed,
        out_specs=(P("band", "pw", None, None), P(None, "pw", "band", None)),
        check_vma=False,
    )
```

```python
import math

import jax
import jax.numpy as jnp
from jax import lax
from jax.sharding import PartitionSpec as P

SENT = 1
CHUNKS = 4

exact_share = 0.25
spacing = 0.2
highest = lax.Precision.HIGHEST


def dft_tables(length, number):
    samples = lax.optimization_barrier(jnp.arange(length, dtype=jnp.int32))
    frequency = jnp.arange(number, dtype=jnp.int32)
    phase_index = samples[:, None] * frequency[None, :] % length
    phase_angle = phase_index.astype(jnp.float32) * (2 * math.pi / length)
    return (jnp.cos(phase_angle), jnp.sin(phase_angle))


def signed(freq, length):
    return jnp.where(freq > length // 2, freq - length, freq)


def coulomb_table(nx, ny, nz, ky_first, rows_y, kz_first, cols_z):
    freq_x = signed(jnp.arange(nx, dtype=jnp.int32), nx)
    freq_y = signed(ky_first + jnp.arange(rows_y, dtype=jnp.int32), ny)
    freq_z = signed(kz_first + jnp.arange(cols_z, dtype=jnp.int32), nz)
    wave_x = freq_x.astype(jnp.float32) * (2 * math.pi / (nx * spacing))
    wave_y = freq_y.astype(jnp.float32) * (2 * math.pi / (ny * spacing))
    wave_z = freq_z.astype(jnp.float32) * (2 * math.pi / (nz * spacing))
    square = (
        (wave_x * wave_x)[:, None, None]
        + (wave_y * wave_y)[None, :, None]
        + (wave_z * wave_z)[None, None, :]
    )
    safe = jnp.where(square > 0, square, 1.0)
    return jnp.where(square > 0, 4 * math.pi / safe, 0.0)


def complex_pass(spectrum, cosine_table, sine_table, pattern, direction):
    half_width = spectrum.shape[-1] // 2
    with_cosine = jnp.einsum(pattern, cosine_table, spectrum, precision=highest)
    with_sine = jnp.einsum(pattern, sine_table, spectrum, precision=highest)
    real_part = with_cosine[..., :half_width] + direction * with_sine[..., half_width:]
    imag_part = with_cosine[..., half_width:] - direction * with_sine[..., :half_width]
    return jnp.concatenate([real_part, imag_part], -1)


def band_broadcast(block, owner, groups):
    rows = block.shape[0] * block.shape[1]
    pieces = block.reshape(groups, rows // groups, block.shape[2])
    received = lax.all_to_all(pieces, "band", 0, 0, tiled=True)
    mine = lax.dynamic_index_in_dim(received, owner, 0, keepdims=True)
    spread = jnp.broadcast_to(mine, pieces.shape)
    gathered = lax.all_to_all(spread, "band", 0, 0, tiled=True)
    return gathered.reshape(block.shape)


def band_reduce_scatter(partial, groups):
    slab_rows, ny, nz = partial.shape
    rows = ny // groups
    pieces = partial.reshape(slab_rows, groups, rows, nz).transpose(1, 0, 2, 3)
    pieces = pieces.reshape(groups, slab_rows * rows, nz)
    received = lax.all_to_all(pieces, "band", 0, 0, tiled=True)
    return jnp.sum(received, 0).reshape(slab_rows, rows, nz)


def on_device(orbitals, owner_group):
    slab_rows, ny, nz = orbitals.shape[1:]
    pw_size = lax.axis_size("pw")
    groups = lax.axis_size("band")
    nx = slab_rows * pw_size
    rows_y = ny // pw_size
    ky_first = lax.axis_index("pw") * rows_y
    width = nz // CHUNKS

    sent_values = band_broadcast(orbitals[0], owner_group[0], groups).astype(jnp.float32)
    own_values = orbitals.astype(jnp.float32)
    packed = jnp.concatenate(
        [own_values[0] * sent_values, own_values[1] * sent_values], -1
    )

    cosine_z, sine_z = dft_tables(nz, nz)
    forward_z = jnp.concatenate(
        [jnp.concatenate([cosine_z, -sine_z], 1), jnp.concatenate([sine_z, cosine_z], 1)], 0
    )
    scale = 1.0 / (nx * ny * nz)
    inverse_z = jnp.concatenate(
        [jnp.concatenate([cosine_z, sine_z], 1), jnp.concatenate([-sine_z, cosine_z], 1)], 0
    ) * scale
    cosine_y, sine_y = dft_tables(ny, ny)
    cosine_x, sine_x = dft_tables(nx, nx)

    result = None
    for chunk in range(CHUNKS):
        low = chunk * width
        columns = jnp.concatenate(
            [forward_z[:, low : low + width], forward_z[:, nz + low : nz + low + width]], 1
        )
        spectrum = jnp.einsum("xyz,zc->xyc", packed, columns, precision=highest)
        spectrum = complex_pass(spectrum, cosine_y, sine_y, "uy,xyc->xuc", 1.0)
        spectrum = lax.all_to_all(spectrum, "pw", 1, 0, tiled=True)
        spectrum = complex_pass(spectrum, cosine_x, sine_x, "ux,xyc->uyc", 1.0)
        kernel = coulomb_table(nx, ny, nz, ky_first, rows_y, low, width)
        spectrum = spectrum * jnp.concatenate([kernel, kernel], -1)
        spectrum = complex_pass(spectrum, cosine_x, sine_x, "ux,xyc->uyc", -1.0)
        spectrum = lax.all_to_all(spectrum, "pw", 0, 1, tiled=True)
        spectrum = complex_pass(spectrum, cosine_y, sine_y, "uy,xyc->xuc", -1.0)
        rows = jnp.concatenate(
            [inverse_z[low : low + width], inverse_z[nz + low : nz + low + width]], 0
        )
        part = jnp.einsum("xyc,cz->xyz", spectrum, rows, precision=highest)
        result = part if result is None else result + part

    potential = jnp.stack([result[..., :nz], result[..., nz:]])
    exchange_rows = -exact_share * (potential * sent_values[None])
    partial_value = -exact_share * jnp.sum(potential * own_values, 0)
    owner_update = band_reduce_scatter(partial_value, groups)[None]
    return (exchange_rows, owner_update)


def solution(mesh):
    placed = (P("band", "pw", None, None), P())
    return jax.shard_map(
        on_device,
        mesh=mesh,
        in_specs=placed,
        out_specs=(P("band", "pw", None, None), P(None, "pw", "band", None)),
        check_vma=False,
    )
```

```python
import math

import jax
import jax.numpy as jnp
from jax import lax
from jax.sharding import PartitionSpec as P

SENT = 1
CHUNKS = 4

exact_share = 0.25
spacing = 0.2
highest = lax.Precision.HIGHEST


def dft_tables(length, number):
    samples = lax.optimization_barrier(jnp.arange(length, dtype=jnp.int32))
    frequency = jnp.arange(number, dtype=jnp.int32)
    phase_index = samples[:, None] * frequency[None, :] % length
    phase_angle = phase_index.astype(jnp.float32) * (2 * math.pi / length)
    return (jnp.cos(phase_angle), jnp.sin(phase_angle))


def signed(freq, length):
    return jnp.where(freq > length // 2, freq - length, freq)


def coulomb_table(nx, ny, nz, ky_first, rows_y, kz_first, cols_z):
    freq_x = signed(jnp.arange(nx, dtype=jnp.int32), nx)
    freq_y = signed(ky_first + jnp.arange(rows_y, dtype=jnp.int32), ny)
    freq_z = signed(kz_first + jnp.arange(cols_z, dtype=jnp.int32), nz)
    wave_x = freq_x.astype(jnp.float32) * (2 * math.pi / (nx * spacing))
    wave_y = freq_y.astype(jnp.float32) * (2 * math.pi / (ny * spacing))
    wave_z = freq_z.astype(jnp.float32) * (2 * math.pi / (nz * spacing))
    square = (
        (wave_x * wave_x)[:, None, None]
        + (wave_y * wave_y)[None, :, None]
        + (wave_z * wave_z)[None, None, :]
    )
    safe = jnp.where(square > 0, square, 1.0)
    return jnp.where(square > 0, 4 * math.pi / safe, 0.0)


def complex_pass(spectrum, cosine_table, sine_table, pattern, direction):
    half_width = spectrum.shape[-1] // 2
    with_cosine = jnp.einsum(pattern, cosine_table, spectrum, precision=highest)
    with_sine = jnp.einsum(pattern, sine_table, spectrum, precision=highest)
    real_part = with_cosine[..., :half_width] + direction * with_sine[..., half_width:]
    imag_part = with_cosine[..., half_width:] - direction * with_sine[..., :half_width]
    return jnp.concatenate([real_part, imag_part], -1)


def band_broadcast(block, owner, groups):
    rows = block.shape[0] * block.shape[1]
    pieces = block.reshape(groups, rows // groups, block.shape[2])
    me = lax.axis_index("band")

    def from_source(source):
        def run(pieces):
            total = jnp.where(me == source, pieces[source], jnp.zeros_like(pieces[source]))
            for target in range(groups):
                if target != source:
                    total = total + lax.ppermute(pieces[target], "band", [(source, target)])
            return total

        return run

    mine = lax.switch(owner, [from_source(source) for source in range(groups)], pieces)
    spread = jnp.broadcast_to(mine[None], pieces.shape)
    gathered = lax.all_to_all(spread, "band", 0, 0, tiled=True)
    return gathered.reshape(block.shape)


def band_reduce_scatter(partial, groups):
    slab_rows, ny, nz = partial.shape
    rows = ny // groups
    pieces = partial.reshape(slab_rows, groups, rows, nz).transpose(1, 0, 2, 3)
    pieces = pieces.reshape(groups, slab_rows * rows, nz)
    received = lax.all_to_all(pieces, "band", 0, 0, tiled=True)
    return jnp.sum(received, 0).reshape(slab_rows, rows, nz)


def on_device(orbitals, owner_group):
    slab_rows, ny, nz = orbitals.shape[1:]
    pw_size = lax.axis_size("pw")
    groups = lax.axis_size("band")
    nx = slab_rows * pw_size
    rows_y = ny // pw_size
    ky_first = lax.axis_index("pw") * rows_y
    width = nz // CHUNKS

    sent_values = band_broadcast(orbitals[0], owner_group[0], groups).astype(jnp.float32)
    own_values = orbitals.astype(jnp.float32)
    packed = jnp.concatenate(
        [own_values[0] * sent_values, own_values[1] * sent_values], -1
    )

    cosine_z, sine_z = dft_tables(nz, nz)
    forward_z = jnp.concatenate(
        [jnp.concatenate([cosine_z, -sine_z], 1), jnp.concatenate([sine_z, cosine_z], 1)], 0
    )
    scale = 1.0 / (nx * ny * nz)
    inverse_z = jnp.concatenate(
        [jnp.concatenate([cosine_z, sine_z], 1), jnp.concatenate([-sine_z, cosine_z], 1)], 0
    ) * scale
    cosine_y, sine_y = dft_tables(ny, ny)
    cosine_x, sine_x = dft_tables(nx, nx)

    result = None
    for chunk in range(CHUNKS):
        low = chunk * width
        columns = jnp.concatenate(
            [forward_z[:, low : low + width], forward_z[:, nz + low : nz + low + width]], 1
        )
        spectrum = jnp.einsum("xyz,zc->xyc", packed, columns, precision=highest)
        spectrum = complex_pass(spectrum, cosine_y, sine_y, "uy,xyc->xuc", 1.0)
        spectrum = lax.all_to_all(spectrum, "pw", 1, 0, tiled=True)
        spectrum = complex_pass(spectrum, cosine_x, sine_x, "ux,xyc->uyc", 1.0)
        kernel = coulomb_table(nx, ny, nz, ky_first, rows_y, low, width)
        spectrum = spectrum * jnp.concatenate([kernel, kernel], -1)
        spectrum = complex_pass(spectrum, cosine_x, sine_x, "ux,xyc->uyc", -1.0)
        spectrum = lax.all_to_all(spectrum, "pw", 0, 1, tiled=True)
        spectrum = complex_pass(spectrum, cosine_y, sine_y, "uy,xyc->xuc", -1.0)
        rows = jnp.concatenate(
            [inverse_z[low : low + width], inverse_z[nz + low : nz + low + width]], 0
        )
        part = jnp.einsum("xyc,cz->xyz", spectrum, rows, precision=highest)
        result = part if result is None else result + part

    potential = jnp.stack([result[..., :nz], result[..., nz:]])
    exchange_rows = -exact_share * (potential * sent_values[None])
    partial_value = -exact_share * jnp.sum(potential * own_values, 0)
    owner_update = band_reduce_scatter(partial_value, groups)[None]
    return (exchange_rows, owner_update)


def solution(mesh):
    placed = (P("band", "pw", None, None), P())
    return jax.shard_map(
        on_device,
        mesh=mesh,
        in_specs=placed,
        out_specs=(P("band", "pw", None, None), P(None, "pw", "band", None)),
        check_vma=False,
    )
```

```python
import math

import jax
import jax.numpy as jnp
from jax import lax
from jax.sharding import PartitionSpec as P

SENT = 1
CHUNKS = 4

exact_share = 0.25
spacing = 0.2
highest = lax.Precision.HIGHEST


def dft_tables(length, number):
    samples = lax.optimization_barrier(jnp.arange(length, dtype=jnp.int32))
    frequency = jnp.arange(number, dtype=jnp.int32)
    phase_index = samples[:, None] * frequency[None, :] % length
    phase_angle = phase_index.astype(jnp.float32) * (2 * math.pi / length)
    return (jnp.cos(phase_angle), jnp.sin(phase_angle))


def signed(freq, length):
    return jnp.where(freq > length // 2, freq - length, freq)


def coulomb_table(nx, ny, nz, ky_first, rows_y, kz_first, cols_z):
    freq_x = signed(jnp.arange(nx, dtype=jnp.int32), nx)
    freq_y = signed(ky_first + jnp.arange(rows_y, dtype=jnp.int32), ny)
    freq_z = signed(kz_first + jnp.arange(cols_z, dtype=jnp.int32), nz)
    wave_x = freq_x.astype(jnp.float32) * (2 * math.pi / (nx * spacing))
    wave_y = freq_y.astype(jnp.float32) * (2 * math.pi / (ny * spacing))
    wave_z = freq_z.astype(jnp.float32) * (2 * math.pi / (nz * spacing))
    square = (
        (wave_x * wave_x)[:, None, None]
        + (wave_y * wave_y)[None, :, None]
        + (wave_z * wave_z)[None, None, :]
    )
    safe = jnp.where(square > 0, square, 1.0)
    return jnp.where(square > 0, 4 * math.pi / safe, 0.0)


def complex_pass(spectrum, cosine_table, sine_table, pattern, direction):
    half_width = spectrum.shape[-1] // 2
    with_cosine = jnp.einsum(pattern, cosine_table, spectrum, precision=highest)
    with_sine = jnp.einsum(pattern, sine_table, spectrum, precision=highest)
    real_part = with_cosine[..., :half_width] + direction * with_sine[..., half_width:]
    imag_part = with_cosine[..., half_width:] - direction * with_sine[..., :half_width]
    return jnp.concatenate([real_part, imag_part], -1)


def band_broadcast(block, owner, groups):
    rows = block.shape[0] * block.shape[1]
    pieces = block.reshape(groups, rows // groups, block.shape[2])
    received = lax.all_to_all(pieces, "band", 0, 0, tiled=True)
    mine = lax.dynamic_index_in_dim(received, owner, 0, keepdims=True)
    spread = jnp.broadcast_to(mine, pieces.shape)
    gathered = lax.all_to_all(spread, "band", 0, 0, tiled=True)
    return gathered.reshape(block.shape)


def band_reduce_scatter(partial, groups):
    slab_rows, ny, nz = partial.shape
    rows = ny // groups
    pieces = partial.reshape(slab_rows, groups, rows, nz).transpose(1, 0, 2, 3)
    pieces = pieces.reshape(groups, slab_rows * rows, nz)
    received = lax.all_to_all(pieces, "band", 0, 0, tiled=True)
    return jnp.sum(received, 0).reshape(slab_rows, rows, nz)


def on_device(orbitals, owner_group):
    slab_rows, ny, nz = orbitals.shape[1:]
    pw_size = lax.axis_size("pw")
    groups = lax.axis_size("band")
    nx = slab_rows * pw_size
    rows_y = ny // pw_size
    ky_first = lax.axis_index("pw") * rows_y
    width = nz // CHUNKS

    sent_values = band_broadcast(orbitals[0], owner_group[0], groups).astype(jnp.float32)
    own_values = orbitals.astype(jnp.float32)
    packed = jnp.concatenate(
        [own_values[0] * sent_values, own_values[1] * sent_values], -1
    )

    cosine_z, sine_z = dft_tables(nz, nz)
    forward_z = jnp.concatenate(
        [jnp.concatenate([cosine_z, -sine_z], 1), jnp.concatenate([sine_z, cosine_z], 1)], 0
    )
    scale = 1.0 / (nx * ny * nz)
    inverse_z = jnp.concatenate(
        [jnp.concatenate([cosine_z, sine_z], 1), jnp.concatenate([-sine_z, cosine_z], 1)], 0
    ) * scale
    cosine_y, sine_y = dft_tables(ny, ny)
    cosine_x, sine_x = dft_tables(nx, nx)

    result = None
    for chunk in range(CHUNKS):
        low = chunk * width
        columns = jnp.concatenate(
            [forward_z[:, low : low + width], forward_z[:, nz + low : nz + low + width]], 1
        )
        spectrum = jnp.einsum("xyz,zc->xyc", packed, columns, precision=highest)
        spectrum = complex_pass(spectrum, cosine_y, sine_y, "uy,xyc->xuc", 1.0)
        spectrum = lax.all_to_all(spectrum, "pw", 1, 1, tiled=True)
        spectrum = spectrum.reshape(slab_rows, pw_size, rows_y, 2 * width)
        spectrum = spectrum.transpose(1, 0, 2, 3).reshape(nx, rows_y, 2 * width)
        spectrum = complex_pass(spectrum, cosine_x, sine_x, "ux,xyc->uyc", 1.0)
        kernel = coulomb_table(nx, ny, nz, ky_first, rows_y, low, width)
        spectrum = spectrum * jnp.concatenate([kernel, kernel], -1)
        spectrum = complex_pass(spectrum, cosine_x, sine_x, "ux,xyc->yuc", -1.0)
        spectrum = lax.all_to_all(spectrum, "pw", 1, 1, tiled=True)
        spectrum = spectrum.reshape(rows_y, pw_size, slab_rows, 2 * width)
        spectrum = spectrum.transpose(2, 1, 0, 3).reshape(slab_rows, ny, 2 * width)
        spectrum = complex_pass(spectrum, cosine_y, sine_y, "uy,xyc->xuc", -1.0)
        rows = jnp.concatenate(
            [inverse_z[low : low + width], inverse_z[nz + low : nz + low + width]], 0
        )
        part = jnp.einsum("xyc,cz->xyz", spectrum, rows, precision=highest)
        result = part if result is None else result + part

    potential = jnp.stack([result[..., :nz], result[..., nz:]])
    exchange_rows = -exact_share * (potential * sent_values[None])
    partial_value = -exact_share * jnp.sum(potential * own_values, 0)
    owner_update = band_reduce_scatter(partial_value, groups)[None]
    return (exchange_rows, owner_update)


def solution(mesh):
    placed = (P("band", "pw", None, None), P())
    return jax.shard_map(
        on_device,
        mesh=mesh,
        in_specs=placed,
        out_specs=(P("band", "pw", None, None), P(None, "pw", "band", None)),
        check_vma=False,
    )
```

```python
import math

import jax
import jax.numpy as jnp
from jax import lax
from jax.sharding import PartitionSpec as P

SENT = 1
CHUNKS = 2

exact_share = 0.25
spacing = 0.2
highest = lax.Precision.HIGHEST


def dft_tables(length, number):
    samples = lax.optimization_barrier(jnp.arange(length, dtype=jnp.int32))
    frequency = jnp.arange(number, dtype=jnp.int32)
    phase_index = samples[:, None] * frequency[None, :] % length
    phase_angle = phase_index.astype(jnp.float32) * (2 * math.pi / length)
    return (jnp.cos(phase_angle), jnp.sin(phase_angle))


def signed(freq, length):
    return jnp.where(freq > length // 2, freq - length, freq)


def coulomb_table(nx, ny, nz, ky_first, rows_y, kz_first, cols_z):
    freq_x = signed(jnp.arange(nx, dtype=jnp.int32), nx)
    freq_y = signed(ky_first + jnp.arange(rows_y, dtype=jnp.int32), ny)
    freq_z = signed(kz_first + jnp.arange(cols_z, dtype=jnp.int32), nz)
    wave_x = freq_x.astype(jnp.float32) * (2 * math.pi / (nx * spacing))
    wave_y = freq_y.astype(jnp.float32) * (2 * math.pi / (ny * spacing))
    wave_z = freq_z.astype(jnp.float32) * (2 * math.pi / (nz * spacing))
    square = (
        (wave_x * wave_x)[:, None, None]
        + (wave_y * wave_y)[None, :, None]
        + (wave_z * wave_z)[None, None, :]
    )
    safe = jnp.where(square > 0, square, 1.0)
    return jnp.where(square > 0, 4 * math.pi / safe, 0.0)


def complex_pass(spectrum, cosine_table, sine_table, pattern, direction):
    half_width = spectrum.shape[-1] // 2
    with_cosine = jnp.einsum(pattern, cosine_table, spectrum, precision=highest)
    with_sine = jnp.einsum(pattern, sine_table, spectrum, precision=highest)
    real_part = with_cosine[..., :half_width] + direction * with_sine[..., half_width:]
    imag_part = with_cosine[..., half_width:] - direction * with_sine[..., :half_width]
    return jnp.concatenate([real_part, imag_part], -1)


def band_broadcast(block, owner, groups):
    rows = block.shape[0] * block.shape[1]
    pieces = block.reshape(groups, rows // groups, block.shape[2])
    received = lax.all_to_all(pieces, "band", 0, 0, tiled=True)
    mine = lax.dynamic_index_in_dim(received, owner, 0, keepdims=True)
    spread = jnp.broadcast_to(mine, pieces.shape)
    gathered = lax.all_to_all(spread, "band", 0, 0, tiled=True)
    return gathered.reshape(block.shape)


def band_reduce_scatter(partial, groups):
    slab_rows, ny, nz = partial.shape
    rows = ny // groups
    pieces = partial.reshape(slab_rows, groups, rows, nz).transpose(1, 0, 2, 3)
    pieces = pieces.reshape(groups, slab_rows * rows, nz)
    received = lax.all_to_all(pieces, "band", 0, 0, tiled=True)
    return jnp.sum(received, 0).reshape(slab_rows, rows, nz)


def on_device(orbitals, owner_group):
    slab_rows, ny, nz = orbitals.shape[1:]
    pw_size = lax.axis_size("pw")
    groups = lax.axis_size("band")
    nx = slab_rows * pw_size
    rows_y = ny // pw_size
    ky_first = lax.axis_index("pw") * rows_y
    width = nz // CHUNKS

    sent_values = band_broadcast(orbitals[0], owner_group[0], groups).astype(jnp.float32)
    own_values = orbitals.astype(jnp.float32)
    packed = jnp.concatenate(
        [own_values[0] * sent_values, own_values[1] * sent_values], -1
    )

    cosine_z, sine_z = dft_tables(nz, nz)
    forward_z = jnp.concatenate(
        [jnp.concatenate([cosine_z, -sine_z], 1), jnp.concatenate([sine_z, cosine_z], 1)], 0
    )
    scale = 1.0 / (nx * ny * nz)
    inverse_z = jnp.concatenate(
        [jnp.concatenate([cosine_z, sine_z], 1), jnp.concatenate([-sine_z, cosine_z], 1)], 0
    ) * scale
    cosine_y, sine_y = dft_tables(ny, ny)
    cosine_x, sine_x = dft_tables(nx, nx)

    result = None
    for chunk in range(CHUNKS):
        low = chunk * width
        columns = jnp.concatenate(
            [forward_z[:, low : low + width], forward_z[:, nz + low : nz + low + width]], 1
        )
        spectrum = jnp.einsum("xyz,zc->xyc", packed, columns, precision=highest)
        spectrum = complex_pass(spectrum, cosine_y, sine_y, "uy,xyc->xuc", 1.0)
        spectrum = lax.all_to_all(spectrum, "pw", 1, 0, tiled=True)
        spectrum = complex_pass(spectrum, cosine_x, sine_x, "ux,xyc->uyc", 1.0)
        kernel = coulomb_table(nx, ny, nz, ky_first, rows_y, low, width)
        spectrum = spectrum * jnp.concatenate([kernel, kernel], -1)
        spectrum = complex_pass(spectrum, cosine_x, sine_x, "ux,xyc->uyc", -1.0)
        spectrum = lax.all_to_all(spectrum, "pw", 0, 1, tiled=True)
        spectrum = complex_pass(spectrum, cosine_y, sine_y, "uy,xyc->xuc", -1.0)
        rows = jnp.concatenate(
            [inverse_z[low : low + width], inverse_z[nz + low : nz + low + width]], 0
        )
        part = jnp.einsum("xyc,cz->xyz", spectrum, rows, precision=highest)
        result = part if result is None else result + part

    potential = jnp.stack([result[..., :nz], result[..., nz:]])
    exchange_rows = -exact_share * (potential * sent_values[None])
    partial_value = -exact_share * jnp.sum(potential * own_values, 0)
    owner_update = band_reduce_scatter(partial_value, groups)[None]
    return (exchange_rows, owner_update)


def solution(mesh):
    placed = (P("band", "pw", None, None), P())
    return jax.shard_map(
        on_device,
        mesh=mesh,
        in_specs=placed,
        out_specs=(P("band", "pw", None, None), P(None, "pw", "band", None)),
        check_vma=False,
    )
```

```python
import math

import jax
import jax.numpy as jnp
from jax import lax
from jax.sharding import PartitionSpec as P

SENT = 1
CHUNKS = 1

exact_share = 0.25
spacing = 0.2
highest = lax.Precision.HIGHEST


def dft_tables(length, number):
    samples = lax.optimization_barrier(jnp.arange(length, dtype=jnp.int32))
    frequency = jnp.arange(number, dtype=jnp.int32)
    phase_index = samples[:, None] * frequency[None, :] % length
    phase_angle = phase_index.astype(jnp.float32) * (2 * math.pi / length)
    return (jnp.cos(phase_angle), jnp.sin(phase_angle))


def signed(freq, length):
    return jnp.where(freq > length // 2, freq - length, freq)


def coulomb_table(nx, ny, nz, ky_first, rows_y, kz_first, cols_z):
    freq_x = signed(jnp.arange(nx, dtype=jnp.int32), nx)
    freq_y = signed(ky_first + jnp.arange(rows_y, dtype=jnp.int32), ny)
    freq_z = signed(kz_first + jnp.arange(cols_z, dtype=jnp.int32), nz)
    wave_x = freq_x.astype(jnp.float32) * (2 * math.pi / (nx * spacing))
    wave_y = freq_y.astype(jnp.float32) * (2 * math.pi / (ny * spacing))
    wave_z = freq_z.astype(jnp.float32) * (2 * math.pi / (nz * spacing))
    square = (
        (wave_x * wave_x)[:, None, None]
        + (wave_y * wave_y)[None, :, None]
        + (wave_z * wave_z)[None, None, :]
    )
    safe = jnp.where(square > 0, square, 1.0)
    return jnp.where(square > 0, 4 * math.pi / safe, 0.0)


def complex_pass(spectrum, cosine_table, sine_table, pattern, direction):
    half_width = spectrum.shape[-1] // 2
    with_cosine = jnp.einsum(pattern, cosine_table, spectrum, precision=highest)
    with_sine = jnp.einsum(pattern, sine_table, spectrum, precision=highest)
    real_part = with_cosine[..., :half_width] + direction * with_sine[..., half_width:]
    imag_part = with_cosine[..., half_width:] - direction * with_sine[..., :half_width]
    return jnp.concatenate([real_part, imag_part], -1)


def band_broadcast(block, owner, groups):
    rows = block.shape[0] * block.shape[1]
    pieces = block.reshape(groups, rows // groups, block.shape[2])
    received = lax.all_to_all(pieces, "band", 0, 0, tiled=True)
    mine = lax.dynamic_index_in_dim(received, owner, 0, keepdims=True)
    spread = jnp.broadcast_to(mine, pieces.shape)
    gathered = lax.all_to_all(spread, "band", 0, 0, tiled=True)
    return gathered.reshape(block.shape)


def band_reduce_scatter(partial, groups):
    slab_rows, ny, nz = partial.shape
    rows = ny // groups
    pieces = partial.reshape(slab_rows, groups, rows, nz).transpose(1, 0, 2, 3)
    pieces = pieces.reshape(groups, slab_rows * rows, nz)
    received = lax.all_to_all(pieces, "band", 0, 0, tiled=True)
    return jnp.sum(received, 0).reshape(slab_rows, rows, nz)


def on_device(orbitals, owner_group):
    slab_rows, ny, nz = orbitals.shape[1:]
    pw_size = lax.axis_size("pw")
    groups = lax.axis_size("band")
    nx = slab_rows * pw_size
    rows_y = ny // pw_size
    ky_first = lax.axis_index("pw") * rows_y
    width = nz // CHUNKS

    sent_values = band_broadcast(orbitals[0], owner_group[0], groups).astype(jnp.float32)
    own_values = orbitals.astype(jnp.float32)
    packed = jnp.concatenate(
        [own_values[0] * sent_values, own_values[1] * sent_values], -1
    )

    cosine_z, sine_z = dft_tables(nz, nz)
    forward_z = jnp.concatenate(
        [jnp.concatenate([cosine_z, -sine_z], 1), jnp.concatenate([sine_z, cosine_z], 1)], 0
    )
    scale = 1.0 / (nx * ny * nz)
    inverse_z = jnp.concatenate(
        [jnp.concatenate([cosine_z, sine_z], 1), jnp.concatenate([-sine_z, cosine_z], 1)], 0
    ) * scale
    cosine_y, sine_y = dft_tables(ny, ny)
    cosine_x, sine_x = dft_tables(nx, nx)

    result = None
    for chunk in range(CHUNKS):
        low = chunk * width
        columns = jnp.concatenate(
            [forward_z[:, low : low + width], forward_z[:, nz + low : nz + low + width]], 1
        )
        spectrum = jnp.einsum("xyz,zc->xyc", packed, columns, precision=highest)
        spectrum = complex_pass(spectrum, cosine_y, sine_y, "uy,xyc->xuc", 1.0)
        spectrum = lax.all_to_all(spectrum, "pw", 1, 0, tiled=True)
        spectrum = complex_pass(spectrum, cosine_x, sine_x, "ux,xyc->uyc", 1.0)
        kernel = coulomb_table(nx, ny, nz, ky_first, rows_y, low, width)
        spectrum = spectrum * jnp.concatenate([kernel, kernel], -1)
        spectrum = complex_pass(spectrum, cosine_x, sine_x, "ux,xyc->uyc", -1.0)
        spectrum = lax.all_to_all(spectrum, "pw", 0, 1, tiled=True)
        spectrum = complex_pass(spectrum, cosine_y, sine_y, "uy,xyc->xuc", -1.0)
        rows = jnp.concatenate(
            [inverse_z[low : low + width], inverse_z[nz + low : nz + low + width]], 0
        )
        part = jnp.einsum("xyc,cz->xyz", spectrum, rows, precision=highest)
        result = part if result is None else result + part

    potential = jnp.stack([result[..., :nz], result[..., nz:]])
    exchange_rows = -exact_share * (potential * sent_values[None])
    partial_value = -exact_share * jnp.sum(potential * own_values, 0)
    owner_update = band_reduce_scatter(partial_value, groups)[None]
    return (exchange_rows, owner_update)


def solution(mesh):
    placed = (P("band", "pw", None, None), P())
    return jax.shard_map(
        on_device,
        mesh=mesh,
        in_specs=placed,
        out_specs=(P("band", "pw", None, None), P(None, "pw", "band", None)),
        check_vma=False,
    )
```

```python
import math

import jax
import jax.numpy as jnp
from jax import lax
from jax.sharding import PartitionSpec as P

SENT = 1
CHUNKS = 2

exact_share = 0.25
spacing = 0.2
highest = lax.Precision.HIGHEST


def dft_tables(length, number):
    samples = lax.optimization_barrier(jnp.arange(length, dtype=jnp.int32))
    frequency = jnp.arange(number, dtype=jnp.int32)
    phase_index = samples[:, None] * frequency[None, :] % length
    phase_angle = phase_index.astype(jnp.float32) * (2 * math.pi / length)
    return (jnp.cos(phase_angle), jnp.sin(phase_angle))


def signed(freq, length):
    return jnp.where(freq > length // 2, freq - length, freq)


def coulomb_table(nx, ny, nz, ky_first, rows_y, kz_first, cols_z):
    freq_x = signed(jnp.arange(nx, dtype=jnp.int32), nx)
    freq_y = signed(ky_first + jnp.arange(rows_y, dtype=jnp.int32), ny)
    freq_z = signed(kz_first + jnp.arange(cols_z, dtype=jnp.int32), nz)
    wave_x = freq_x.astype(jnp.float32) * (2 * math.pi / (nx * spacing))
    wave_y = freq_y.astype(jnp.float32) * (2 * math.pi / (ny * spacing))
    wave_z = freq_z.astype(jnp.float32) * (2 * math.pi / (nz * spacing))
    square = (
        (wave_x * wave_x)[:, None, None]
        + (wave_y * wave_y)[None, :, None]
        + (wave_z * wave_z)[None, None, :]
    )
    safe = jnp.where(square > 0, square, 1.0)
    return jnp.where(square > 0, 4 * math.pi / safe, 0.0)


def complex_pass(spectrum, cosine_table, sine_table, pattern, direction):
    half_width = spectrum.shape[-1] // 2
    with_cosine = jnp.einsum(pattern, cosine_table, spectrum, precision=highest)
    with_sine = jnp.einsum(pattern, sine_table, spectrum, precision=highest)
    real_part = with_cosine[..., :half_width] + direction * with_sine[..., half_width:]
    imag_part = with_cosine[..., half_width:] - direction * with_sine[..., :half_width]
    return jnp.concatenate([real_part, imag_part], -1)


def band_broadcast(block, owner, groups):
    rows = block.shape[0] * block.shape[1]
    pieces = block.reshape(groups, rows // groups, block.shape[2])
    received = lax.all_to_all(pieces, "band", 0, 0, tiled=True)
    mine = lax.dynamic_index_in_dim(received, owner, 0, keepdims=True)
    spread = jnp.broadcast_to(mine, pieces.shape)
    gathered = lax.all_to_all(spread, "band", 0, 0, tiled=True)
    return gathered.reshape(block.shape)


def band_reduce_scatter(partial, groups):
    slab_rows, ny, nz = partial.shape
    rows = ny // groups
    pieces = partial.reshape(slab_rows, groups, rows, nz).transpose(1, 0, 2, 3)
    pieces = pieces.reshape(groups, slab_rows * rows, nz)
    received = lax.all_to_all(pieces, "band", 0, 0, tiled=True)
    return jnp.sum(received, 0).reshape(slab_rows, rows, nz)


def on_device(orbitals, owner_group):
    slab_rows, ny, nz = orbitals.shape[1:]
    pw_size = lax.axis_size("pw")
    groups = lax.axis_size("band")
    nx = slab_rows * pw_size
    rows_y = ny // pw_size
    ky_first = lax.axis_index("pw") * rows_y
    width = nz // CHUNKS

    sent_values = band_broadcast(orbitals[0], owner_group[0], groups).astype(jnp.float32)
    own_values = orbitals.astype(jnp.float32)
    packed = jnp.concatenate(
        [own_values[0] * sent_values, own_values[1] * sent_values], -1
    )

    cosine_z, sine_z = dft_tables(nz, nz)
    forward_z = jnp.concatenate(
        [jnp.concatenate([cosine_z, -sine_z], 1), jnp.concatenate([sine_z, cosine_z], 1)], 0
    )
    scale = 1.0 / (nx * ny * nz)
    inverse_z = jnp.concatenate(
        [jnp.concatenate([cosine_z, sine_z], 1), jnp.concatenate([-sine_z, cosine_z], 1)], 0
    ) * scale
    cosine_y, sine_y = dft_tables(ny, ny)
    cosine_x, sine_x = dft_tables(nx, nx)

    result = None
    for chunk in range(CHUNKS):
        low = chunk * width
        columns = jnp.concatenate(
            [forward_z[:, low : low + width], forward_z[:, nz + low : nz + low + width]], 1
        )
        spectrum = jnp.einsum("xyz,zc->xyc", packed, columns, precision=highest)
        spectrum = complex_pass(spectrum, cosine_y, sine_y, "uy,xyc->xuc", 1.0)
        spectrum = lax.all_to_all(spectrum, "pw", 1, 1, tiled=True)
        spectrum = spectrum.reshape(slab_rows, pw_size, rows_y, 2 * width)
        spectrum = spectrum.transpose(1, 0, 2, 3).reshape(nx, rows_y, 2 * width)
        spectrum = complex_pass(spectrum, cosine_x, sine_x, "ux,xyc->uyc", 1.0)
        kernel = coulomb_table(nx, ny, nz, ky_first, rows_y, low, width)
        spectrum = spectrum * jnp.concatenate([kernel, kernel], -1)
        spectrum = complex_pass(spectrum, cosine_x, sine_x, "ux,xyc->yuc", -1.0)
        spectrum = lax.all_to_all(spectrum, "pw", 1, 1, tiled=True)
        spectrum = spectrum.reshape(rows_y, pw_size, slab_rows, 2 * width)
        spectrum = spectrum.transpose(2, 1, 0, 3).reshape(slab_rows, ny, 2 * width)
        spectrum = complex_pass(spectrum, cosine_y, sine_y, "uy,xyc->xuc", -1.0)
        rows = jnp.concatenate(
            [inverse_z[low : low + width], inverse_z[nz + low : nz + low + width]], 0
        )
        part = jnp.einsum("xyc,cz->xyz", spectrum, rows, precision=highest)
        result = part if result is None else result + part

    potential = jnp.stack([result[..., :nz], result[..., nz:]])
    exchange_rows = -exact_share * (potential * sent_values[None])
    partial_value = -exact_share * jnp.sum(potential * own_values, 0)
    owner_update = band_reduce_scatter(partial_value, groups)[None]
    return (exchange_rows, owner_update)


def solution(mesh):
    placed = (P("band", "pw", None, None), P())
    return jax.shard_map(
        on_device,
        mesh=mesh,
        in_specs=placed,
        out_specs=(P("band", "pw", None, None), P(None, "pw", "band", None)),
        check_vma=False,
    )
```

```python
import math

import jax
import jax.numpy as jnp
from jax import lax
from jax.sharding import PartitionSpec as P

SENT = 1
CHUNKS = 2

exact_share = 0.25
spacing = 0.2
highest = lax.Precision.HIGHEST


def dft_tables(length, number):
    samples = lax.optimization_barrier(jnp.arange(length, dtype=jnp.int32))
    frequency = jnp.arange(number, dtype=jnp.int32)
    phase_index = samples[:, None] * frequency[None, :] % length
    phase_angle = phase_index.astype(jnp.float32) * (2 * math.pi / length)
    return (jnp.cos(phase_angle), jnp.sin(phase_angle))


def signed(freq, length):
    return jnp.where(freq > length // 2, freq - length, freq)


def coulomb_table(nx, ny, nz, ky_first, rows_y, kz_first, cols_z):
    freq_x = signed(jnp.arange(nx, dtype=jnp.int32), nx)
    freq_y = signed(ky_first + jnp.arange(rows_y, dtype=jnp.int32), ny)
    freq_z = signed(kz_first + jnp.arange(cols_z, dtype=jnp.int32), nz)
    wave_x = freq_x.astype(jnp.float32) * (2 * math.pi / (nx * spacing))
    wave_y = freq_y.astype(jnp.float32) * (2 * math.pi / (ny * spacing))
    wave_z = freq_z.astype(jnp.float32) * (2 * math.pi / (nz * spacing))
    square = (
        (wave_x * wave_x)[:, None, None]
        + (wave_y * wave_y)[None, :, None]
        + (wave_z * wave_z)[None, None, :]
    )
    safe = jnp.where(square > 0, square, 1.0)
    return jnp.where(square > 0, 4 * math.pi / safe, 0.0)


def complex_pass(spectrum, cosine_table, sine_table, pattern, direction):
    half_width = spectrum.shape[-1] // 2
    with_cosine = jnp.einsum(pattern, cosine_table, spectrum, precision=highest)
    with_sine = jnp.einsum(pattern, sine_table, spectrum, precision=highest)
    real_part = with_cosine[..., :half_width] + direction * with_sine[..., half_width:]
    imag_part = with_cosine[..., half_width:] - direction * with_sine[..., :half_width]
    return jnp.concatenate([real_part, imag_part], -1)


def band_broadcast(block, owner, groups):
    rows = block.shape[0] * block.shape[1]
    pieces = block.reshape(groups, rows // groups, block.shape[2])
    received = lax.all_to_all(pieces, "band", 0, 0, tiled=True)
    mine = lax.dynamic_index_in_dim(received, owner, 0, keepdims=True)
    spread = jnp.broadcast_to(mine, pieces.shape)
    gathered = lax.all_to_all(spread, "band", 0, 0, tiled=True)
    return gathered.reshape(block.shape)


def band_reduce_scatter(partial, groups):
    slab_rows, ny, nz = partial.shape
    rows = ny // groups
    pieces = partial.reshape(slab_rows, groups, rows, nz).transpose(1, 0, 2, 3)
    pieces = pieces.reshape(groups, slab_rows * rows, nz)
    received = lax.all_to_all(pieces, "band", 0, 0, tiled=True)
    return jnp.sum(received, 0).reshape(slab_rows, rows, nz)


def on_device(orbitals, owner_group):
    slab_rows, ny, nz = orbitals.shape[1:]
    pw_size = lax.axis_size("pw")
    groups = lax.axis_size("band")
    nx = slab_rows * pw_size
    rows_y = ny // pw_size
    ky_first = lax.axis_index("pw") * rows_y
    width = nz // CHUNKS

    sent_values = band_broadcast(orbitals[0], owner_group[0], groups).astype(jnp.float32)
    own_values = orbitals.astype(jnp.float32)
    packed = jnp.concatenate(
        [own_values[0] * sent_values, own_values[1] * sent_values], -1
    )

    cosine_z, sine_z = dft_tables(nz, nz)
    forward_z = jnp.concatenate(
        [jnp.concatenate([cosine_z, -sine_z], 1), jnp.concatenate([sine_z, cosine_z], 1)], 0
    )
    scale = 1.0 / (nx * ny * nz)
    inverse_z = jnp.concatenate(
        [jnp.concatenate([cosine_z, sine_z], 1), jnp.concatenate([-sine_z, cosine_z], 1)], 0
    ) * scale
    cosine_y, sine_y = dft_tables(ny, ny)
    cosine_x, sine_x = dft_tables(nx, nx)

    result = None
    for chunk in range(CHUNKS):
        low = chunk * width
        columns = jnp.concatenate(
            [forward_z[:, low : low + width], forward_z[:, nz + low : nz + low + width]], 1
        )
        spectrum = jnp.einsum("xyz,zc->xyc", packed, columns, precision=highest)
        spectrum = complex_pass(spectrum, cosine_y, sine_y, "uy,xyc->xuc", 1.0)
        spectrum = lax.all_to_all(spectrum, "pw", 1, 0, tiled=True)
        spectrum = complex_pass(spectrum, cosine_x, sine_x, "ux,xyc->uyc", 1.0)
        kernel = coulomb_table(nx, ny, nz, ky_first, rows_y, low, width)
        spectrum = spectrum * jnp.concatenate([kernel, kernel], -1)
        spectrum = complex_pass(spectrum, cosine_x, sine_x, "ux,xyc->uyc", -1.0)
        spectrum = lax.all_to_all(spectrum, "pw", 0, 1, tiled=True)
        spectrum = complex_pass(spectrum, cosine_y, sine_y, "uy,xyc->xuc", -1.0)
        rows = jnp.concatenate(
            [inverse_z[low : low + width], inverse_z[nz + low : nz + low + width]], 0
        )
        if chunk < CHUNKS - 1:
            part = jnp.einsum("xyc,cz->xyz", spectrum, rows, precision=highest)
            result = part if result is None else result + part

    half = slab_rows // 2
    rows_out = []
    updates = []
    for first in (0, half):
        planes = slice(first, first + half)
        done = jnp.einsum("xyc,cz->xyz", spectrum[planes], rows, precision=highest)
        if result is not None:
            done = done + result[planes]
        potential = jnp.stack([done[..., :nz], done[..., nz:]])
        rows_out.append(-exact_share * (potential * sent_values[None, planes]))
        partial_value = -exact_share * jnp.sum(potential * own_values[:, planes], 0)
        updates.append(band_reduce_scatter(partial_value, groups))
    exchange_rows = jnp.concatenate(rows_out, 1)
    owner_update = jnp.concatenate(updates, 0)[None]
    return (exchange_rows, owner_update)


def solution(mesh):
    placed = (P("band", "pw", None, None), P())
    return jax.shard_map(
        on_device,
        mesh=mesh,
        in_specs=placed,
        out_specs=(P("band", "pw", None, None), P(None, "pw", "band", None)),
        check_vma=False,
    )
```
